32 devices in a mesh: stratum: 8 (over z, y), tm: 4 (over x, core).
Axes of the slice: x: 2, y: 2, z: 4, core: 2. Of those that a mesh axis runs over, the one named last changes fastest.
Arguments:
- row_factors: float32 [32768, 256], P(('stratum', 'tm')), may hold values from -0.75 to 0.75
- time_factors: float32 [32768, 256], P(('stratum', 'tm')), may hold values from -3 to 3
- values: bfloat16 [2, 32768, 1024], P(None, ('stratum', 'tm')), may hold values from -6 to 6
- tile_mask: int32 [2, 256, 8], P(None, ('stratum', 'tm')), may hold values from 0 to 1, as said below
- lags: int32 [4], replicated, may hold values from 1 to 64, as said below
- ar_weights: float32 [4], replicated, may hold values from -0.4 to 0.4
Outputs:
- rows_out: float32 [32768, 256], P(('stratum', 'tm'))
- time_out: float32 [32768, 256], P(('stratum', 'tm'))
The draws below stay inside these ranges and needn't reach their ends.
Inputs may be any that keep to these rules, and one draw needn't show every extreme that they name: `tile_mask`: 0 or 1; in each sub-epoch each band of 128 series has its own chance of an observed tile, from an eighth to one. `lags`: distinct; the largest is exactly 64.
All inputs are finite; a program needn't handle non-finite values.
Results may differ from the reference program's by a relative error of at most 0.00082.
Values may be sent and summed in bfloat16 or wider, within the bound.
A program may use at most 64 MiB of HBM per device.

```python
import jax
import jax.numpy as jnp
from jax import lax

RANK = 256
RB = 1024
TB = 1024
HALO = 64
LAGS = 4
TILE = 128
SUB = 2
ROWS = 32768
TIMES = 32768
N_STRATUM = 8
N_TM = 4


def draw_tile_mask(key, part):
    first = jax.random.fold_in(key, 11)
    second = jax.random.fold_in(key, 23)
    level = jax.random.randint(first, (SUB, ROWS // TILE, 1), 1, 9)
    ticket = jax.random.randint(second, (SUB, ROWS // TILE, TB // TILE), 0, 8)
    return (ticket < level).astype(jnp.int32)


def draw_lags(key, part):
    picked = jax.random.permutation(jax.random.fold_in(key, 37), HALO - 1)[:LAGS - 1] + 1
    return jnp.concatenate([jnp.array([HALO], jnp.int32), picked.astype(jnp.int32)])


def level_of(stream_key, shape, cuts, smallest, top_value):
    def one(position, parts):
        draws = jax.random.uniform(jax.random.fold_in(jax.random.fold_in(stream_key, 6), position), (parts,), jnp.float32, smallest / len(cuts), top_value / len(cuts))
        return jnp.repeat(jnp.exp(draws), shape[position] // parts).reshape((-1,) + (1,) * (len(shape) - position - 1))

    factor_of = one(*cuts[0])
    for cut in cuts[1:]:
        factor_of = factor_of * one(*cut)
    return factor_of


def bell_draw(stream_key, dims, scale, limit, split=(), held_as=jnp.bfloat16):
    result = scale * jax.random.normal(stream_key, dims, jnp.float32)
    if split:
        result = result * level_of(stream_key, dims, split, -0.22, 0.18)
    return jnp.clip(result, -limit, limit).astype(held_as)


def setup_inputs(seed: int = 0) -> dict:
    key_of = jax.random.split(jax.random.key(seed), 7)
    return {
        "row_factors": bell_draw(key_of[0], (ROWS, RANK), 0.125, 0.75, ((0, 32),), jnp.float32),
        "time_factors": bell_draw(key_of[1], (TIMES, RANK), 0.5, 3.0, ((0, 32),), jnp.float32),
        "values": bell_draw(key_of[2], (SUB, ROWS, TB), 1.0, 6.0, ((1, 32),)),
        "tile_mask": draw_tile_mask(jax.random.fold_in(key_of[6], 71), 0),
        "lags": draw_lags(jax.random.fold_in(key_of[6], 71), 0),
        "ar_weights": jnp.clip(jax.random.uniform(key_of[5], (LAGS,), jnp.float32, -0.4, 0.4), -0.4, 0.4),
    }


rate_rows = 0.005
rate_time = 0.02
ridge_rows = 16.0
ridge_time = 2.0
ridge_lags = 8.0


def block_step(rows, times, observed, marks):
    rows_low = rows.astype(jnp.bfloat16)
    times_low = times.astype(jnp.bfloat16)
    product = jnp.dot(rows_low, times_low.T, preferred_element_type=jnp.float32)
    diff = observed.astype(jnp.float32) - product
    bands = marks.shape[0]
    columns = marks.shape[1]
    spread = diff.reshape(bands, TILE, columns, TILE) * marks.astype(jnp.float32)[:, None, :, None]
    masked = spread.reshape(diff.shape).astype(jnp.bfloat16)
    grad_rows = jnp.dot(masked, times_low, preferred_element_type=jnp.float32)
    grad_time = jnp.dot(masked.T, rows_low, preferred_element_type=jnp.float32)
    return rows + rate_rows * (grad_rows - ridge_rows * rows), grad_time


def reference(row_factors, time_factors, values, tile_mask, lags, ar_weights):
    strata = N_STRATUM
    groups = N_TM
    blocks = strata * groups
    rows_now = row_factors
    time_now = time_factors
    for sweep in range(SUB):
        padded = jnp.pad(time_now, ((HALO, HALO), (0, 0)))
        errors = time_now
        for which in range(LAGS):
            begin = (HALO - lags[which]).astype(jnp.int32)
            errors = errors - ar_weights[which] * lax.dynamic_slice_in_dim(padded, begin, TIMES, 0)
        err_pad = jnp.concatenate([errors, jnp.zeros((HALO, RANK), jnp.float32)], axis=0)
        lag_grad = errors
        for which in range(LAGS):
            begin = lags[which].astype(jnp.int32)
            lag_grad = lag_grad - ar_weights[which] * lax.dynamic_slice_in_dim(err_pad, begin, TIMES, 0)
        row_blocks = rows_now.reshape(blocks, RB, RANK)
        time_blocks = time_now.reshape(blocks, TB, RANK)
        observed = values[sweep].reshape(blocks, RB, TB)
        marks = tile_mask[sweep].reshape(blocks, RB // TILE, TB // TILE)

        def one_block(index):
            owner = ((index // groups + sweep) % strata) * groups + index % groups
            return block_step(row_blocks[owner], time_blocks[index], observed[owner], marks[owner])

        new_rows, grad_time = lax.map(one_block, jnp.arange(blocks, dtype=jnp.int32))
        counter = jnp.arange(blocks, dtype=jnp.int32)
        order = ((counter // groups - sweep) % strata) * groups + counter % groups
        rows_now = jnp.take(new_rows, order, axis=0).reshape(ROWS, RANK)
        time_now = time_now + rate_time * (grad_time.reshape(TIMES, RANK) - ridge_time * time_now - ridge_lags * lag_grad)
    return rows_now, time_now
```

```python
import functools

import jax
import jax.numpy as jnp
from jax import lax
from jax.experimental import pallas as pl
from jax.experimental.pallas import tpu as pltpu
from jax.sharding import PartitionSpec as P

HALO = 64
LAGS = 4
TILE = 128
CHUNK = 256
BAND = 128
PAD = 16
TOP = 32000.0
LOG2_E = 1.4426950408889634

rate_rows = 0.005
rate_time = 0.02
ridge_rows = 16.0
ridge_time = 2.0
ridge_lags = 8.0

MESH = pl.DeviceIdType.MESH
NT = (((1,), (1,)), ((), ()))


def chunk_order(count):
    inner = list(range(1, count - 1))
    return inner + [0, count - 1] if count > 1 else [0]


def kernel(strata, groups, lags, weights, mask, f_hbm, x_hbm, v_hbm, f_out, x_out,
           f, x, v0, v1, r, x1, fb, fbt, xh0, xl0, xh1, xl1, xr, gs, gr, lo0, hi0, lo1, hi1, coef,
           load_sem, out_sem, send_sem, recv_sem, hsend_sem, hrecv_sem):
    block_len = x.shape[0]
    rows = f.shape[0]
    count = block_len // CHUNK
    order = chunk_order(count)
    last = block_len - HALO
    blocks = strata * groups
    s = lax.axis_index("stratum")
    g = lax.axis_index("tm")
    c = s * groups + g
    cr = lax.rem(c + 1, blocks)
    cl = lax.rem(c + blocks - 1, blocks)
    right = (cr // groups, lax.rem(cr, groups))
    left = (cl // groups, lax.rem(cl, groups))
    nxt = (lax.rem(s + 1, strata), g)
    prv = (lax.rem(s + strata - 1, strata), g)

    def cols(j):
        return pl.ds(j * CHUNK, CHUNK)

    def inner(j):
        return pl.ds(HALO + j * CHUNK, CHUNK)

    load_x = pltpu.make_async_copy(x_hbm, x, load_sem.at[0])
    load_f = pltpu.make_async_copy(f_hbm, f, load_sem.at[1])
    load_v1 = pltpu.make_async_copy(v_hbm.at[1], v1, load_sem.at[2])
    load_v0 = {
        j: pltpu.make_async_copy(v_hbm.at[0, :, cols(j)], v0.at[:, cols(j)], load_sem.at[3 + j])
        for j in order
    }
    load_x.start()
    load_f.start()
    for j in order:
        load_v0[j].start()
    load_v1.start()

    barrier = pltpu.get_barrier_semaphore()
    for peer in (left, right, nxt, prv):
        pl.semaphore_signal(barrier, inc=1, device_id=peer, device_id_type=MESH)
    pl.semaphore_wait(barrier, 4)

    def rims(first, final, lo, hi, at):
        to_right = pltpu.make_async_remote_copy(
            src_ref=final, dst_ref=lo, send_sem=hsend_sem.at[at],
            recv_sem=hrecv_sem.at[at], device_id=right, device_id_type=MESH)
        to_left = pltpu.make_async_remote_copy(
            src_ref=first, dst_ref=hi, send_sem=hsend_sem.at[at + 1],
            recv_sem=hrecv_sem.at[at + 1], device_id=left, device_id_type=MESH)
        return to_right, to_left

    rim0_r, rim0_l = rims(x_hbm.at[pl.ds(0, HALO)], x_hbm.at[pl.ds(last, HALO)], lo0, hi0, 0)
    rim1_r, rim1_l = rims(x1.at[pl.ds(0, HALO)], x1.at[pl.ds(last, HALO)], lo1, hi1, 2)
    rim0_r.start()
    rim0_l.start()
    forth = {
        j: pltpu.make_async_remote_copy(
            src_ref=xh1.at[inner(j)], dst_ref=xr.at[cols(j)], send_sem=send_sem.at[j],
            recv_sem=recv_sem.at[j], device_id=nxt, device_id_type=MESH)
        for j in order
    }
    back = {
        j: pltpu.make_async_remote_copy(
            src_ref=gs.at[j], dst_ref=gr.at[j], send_sem=send_sem.at[count + j],
            recv_sem=recv_sem.at[count + j], device_id=prv, device_id_type=MESH)
        for j in order
    }

    lag = [lags[which] for which in range(LAGS)]
    weight = [weights[which] for which in range(LAGS)]
    step = lax.broadcasted_iota(jnp.int32, (BAND, BAND + 2 * HALO), 0)
    offset = lax.broadcasted_iota(jnp.int32, (BAND, BAND + 2 * HALO), 1) - HALO - step
    behind = jnp.where(offset == 0, 1.0, 0.0)
    for which in range(LAGS):
        behind = behind - jnp.where(offset == -lag[which], weight[which], 0.0)
    usual, final = behind, behind
    for which in range(LAGS):
        ahead = jnp.where(offset == lag[which], weight[which], 0.0)
        for other in range(LAGS):
            ahead = ahead - jnp.where(
                offset == lag[which] - lag[other], weight[which] * weight[other], 0.0)
        usual = usual - ahead
        held = (step + lag[which] < BAND) | (c < blocks - 1)
        final = final - jnp.where(held, ahead, 0.0)
    for at, matrix in enumerate((usual, final)):
        high = matrix.astype(jnp.bfloat16)
        coef[2 * at] = high
        coef[2 * at + 1] = (matrix - high.astype(jnp.float32)).astype(jnp.bfloat16)

    def split(value, high_ref, low_ref, at, size):
        high = value.astype(jnp.bfloat16)
        high_ref[pl.ds(at, size), :] = high
        low_ref[pl.ds(at, size), :] = (value - high.astype(jnp.float32)).astype(jnp.bfloat16)

    def rim_low(lo, high_ref, low_ref):
        split(jnp.where(c > 0, lo[...], 0.0), high_ref, low_ref, 0, HALO)

    def rim_high(hi, high_ref, low_ref):
        split(hi[...], high_ref, low_ref, HALO + block_len, HALO)

    def lag_grad(high_ref, low_ref, j):
        bands = []
        for band in range(j * CHUNK // BAND, (j + 1) * CHUNK // BAND):
            near = pl.ds(band * BAND, BAND + 2 * HALO)
            at = 2 if band == block_len // BAND - 1 else 0
            high = high_ref[near, :]
            bands.append(
                jnp.dot(coef[at], high, preferred_element_type=jnp.float32)
                + jnp.dot(coef[at], low_ref[near, :], preferred_element_type=jnp.float32)
                + jnp.dot(coef[at + 1], high, preferred_element_type=jnp.float32))
        return jnp.concatenate(bands, axis=0)

    def chunk_grad(k, j, times, v):
        for band in range(rows // CHUNK):
            product = lax.dot_general(
                fb[pl.ds(band * CHUNK, CHUNK), :], times, NT, preferred_element_type=jnp.float32)
            for i in range(CHUNK // TILE):
                for l in range(CHUNK // TILE):
                    mark = mask[k, band * (CHUNK // TILE) + i, j * (CHUNK // TILE) + l].astype(jnp.float32)
                    here = (pl.ds(band * CHUNK + i * TILE, TILE), pl.ds(j * CHUNK + l * TILE, TILE))
                    tile = product[i * TILE:(i + 1) * TILE, l * TILE:(l + 1) * TILE]
                    r[here] = ((v[here].astype(jnp.float32) - tile) * mark).astype(jnp.bfloat16)
        grad = jnp.dot(fbt[...], r[:, cols(j)], preferred_element_type=jnp.float32)
        return grad.T

    def rows_step(times, base):
        for band in range(rows // CHUNK):
            here = pl.ds(band * CHUNK, CHUNK)
            grad = jnp.dot(
                r[here, :], times[pl.ds(base, block_len), :], preferred_element_type=jnp.float32)
            f[here, :] = f[here, :] + rate_rows * (grad - ridge_rows * f[here, :])

    def round_rows():
        for band in range(rows // CHUNK):
            here = pl.ds(band * CHUNK, CHUNK)
            low = f[here, :].astype(jnp.bfloat16)
            fb[here, :] = low
            fbt[:, here] = low.T

    def pack(grad, j):
        top = jnp.maximum(jnp.max(jnp.abs(grad), axis=0, keepdims=True), 1e-30)
        power = jnp.broadcast_to(jnp.ceil(jnp.log(top) * LOG2_E), (PAD, grad.shape[1]))
        per_unit = TOP * jnp.exp2(-power[:1, :])
        gs[j, pl.ds(0, CHUNK), :] = jnp.floor(grad * per_unit + 0.5).astype(jnp.int32).astype(jnp.int16)
        gs[j, pl.ds(CHUNK, PAD), :] = power.astype(jnp.int32).astype(jnp.int16)

    def unpack(j):
        power = gr[j, pl.ds(CHUNK, PAD), :].astype(jnp.int32).astype(jnp.float32)
        unit = (1.0 / TOP) * jnp.exp2(power[:1, :])
        return gr[j, pl.ds(0, CHUNK), :].astype(jnp.int32).astype(jnp.float32) * unit

    def ridge_step(now, high_ref, low_ref, j):
        return now - rate_time * (ridge_time * now + ridge_lags * lag_grad(high_ref, low_ref, j))

    load_f.wait()
    round_rows()
    load_x.wait()
    for j in range(count):
        split(x[cols(j), :], xh0, xl0, HALO + j * CHUNK, CHUNK)
    for j in order:
        load_v0[j].wait()
        grad = chunk_grad(0, j, xh0[inner(j), :], v0)
        if j == 0:
            rim0_r.wait_recv()
            rim_low(lo0, xh0, xl0)
        if j == count - 1:
            rim0_l.wait_recv()
            rim_high(hi0, xh0, xl0)
        now = ridge_step(x[cols(j), :], xh0, xl0, j) + rate_time * grad
        x1[cols(j), :] = now
        split(now, xh1, xl1, HALO + j * CHUNK, CHUNK)
        forth[j].start()
    rim1_r.start()
    rim1_l.start()
    rows_step(xh0, HALO)
    round_rows()

    load_v1.wait()
    for j in order:
        forth[j].wait_recv()
        grad = chunk_grad(1, j, xr[cols(j), :], v1)
        pack(grad, j)
        back[j].start()
        if j == 0:
            rim1_r.wait_recv()
            rim_low(lo1, xh1, xl1)
        if j == count - 1:
            rim1_l.wait_recv()
            rim_high(hi1, xh1, xl1)
        x[cols(j), :] = ridge_step(x1[cols(j), :], xh1, xl1, j)
    rows_step(xr, 0)
    store_f = pltpu.make_async_copy(f, f_out, out_sem.at[0])
    store_f.start()

    stores = []
    for j in order:
        back[j].wait_recv()
        x[cols(j), :] = x[cols(j), :] + rate_time * unpack(j)
        store = pltpu.make_async_copy(x.at[cols(j)], x_out.at[cols(j)], out_sem.at[1 + j])
        store.start()
        stores.append(store)
    for j in order:
        forth[j].wait_send()
        back[j].wait_send()
    for rim in (rim0_r, rim0_l, rim1_r, rim1_l):
        rim.wait_send()
    store_f.wait()
    for store in stores:
        store.wait()


def body(row_factors, time_factors, values, tile_mask, lags, ar_weights):
    strata = lax.axis_size("stratum")
    groups = lax.axis_size("tm")
    block_len, rank = time_factors.shape
    rows = row_factors.shape[0]
    count = block_len // CHUNK
    f32, bf16 = jnp.float32, jnp.bfloat16
    smem = pl.BlockSpec(memory_space=pltpu.SMEM)
    hbm = pl.BlockSpec(memory_space=pl.ANY)
    return tuple(pl.pallas_call(
        functools.partial(kernel, strata, groups),
        out_shape=(
            jax.ShapeDtypeStruct((rows, rank), f32),
            jax.ShapeDtypeStruct((block_len, rank), f32),
        ),
        in_specs=[smem, smem, smem, hbm, hbm, hbm],
        out_specs=(hbm, hbm),
        scratch_shapes=[
            pltpu.VMEM((rows, rank), f32),
            pltpu.VMEM((block_len, rank), f32),
            pltpu.VMEM((rows, block_len), bf16),
            pltpu.VMEM((rows, block_len), bf16),
            pltpu.VMEM((rows, block_len), bf16),
            pltpu.VMEM((block_len, rank), f32),
            pltpu.VMEM((rows, rank), bf16),
            pltpu.VMEM((rank, rows), bf16),
            pltpu.VMEM((block_len + 2 * HALO, rank), bf16),
            pltpu.VMEM((block_len + 2 * HALO, rank), bf16),
            pltpu.VMEM((block_len + 2 * HALO, rank), bf16),
            pltpu.VMEM((block_len + 2 * HALO, rank), bf16),
            pltpu.VMEM((block_len, rank), bf16),
            pltpu.VMEM((count, CHUNK + PAD, rank), jnp.int16),
            pltpu.VMEM((count, CHUNK + PAD, rank), jnp.int16),
            pltpu.VMEM((HALO, rank), f32),
            pltpu.VMEM((HALO, rank), f32),
            pltpu.VMEM((HALO, rank), f32),
            pltpu.VMEM((HALO, rank), f32),
            pltpu.VMEM((4, BAND, BAND + 2 * HALO), bf16),
            pltpu.SemaphoreType.DMA((3 + count,)),
            pltpu.SemaphoreType.DMA((1 + count,)),
            pltpu.SemaphoreType.DMA((2 * count,)),
            pltpu.SemaphoreType.DMA((2 * count,)),
            pltpu.SemaphoreType.DMA((4,)),
            pltpu.SemaphoreType.DMA((4,)),
        ],
        compiler_params=pltpu.CompilerParams(
            collective_id=0, has_side_effects=True, vmem_limit_bytes=48 * 2**20),
    )(lags, ar_weights, tile_mask, row_factors, time_factors, values))


def solution(mesh):
    return jax.shard_map(
        body,
        mesh=mesh,
        in_specs=(
            P(("stratum", "tm"), None),
            P(("stratum", "tm"), None),
            P(None, ("stratum", "tm"), None),
            P(None, ("stratum", "tm"), None),
            P(),
            P(),
        ),
        out_specs=(P(("stratum", "tm"), None), P(("stratum", "tm"), None)),
        check_vma=False,
    )
```

```python
import functools

import jax
import jax.numpy as jnp
from jax import lax
from jax.experimental import pallas as pl
from jax.experimental.pallas import tpu as pltpu
from jax.sharding import PartitionSpec as P

HALO = 64
LAGS = 4
TILE = 128
CHUNK = 256
BAND = 128
PAD = 16
TOP = 32000.0
LOG2_E = 1.4426950408889634

rate_rows = 0.005
rate_time = 0.02
ridge_rows = 16.0
ridge_time = 2.0
ridge_lags = 8.0

MESH = pl.DeviceIdType.MESH
NT = (((1,), (1,)), ((), ()))


def chunk_order(count):
    inner = list(range(1, count - 1))
    return inner + [0, count - 1] if count > 1 else [0]


def kernel(strata, groups, lags_hbm, weights_hbm, mask_hbm, f_hbm, x_hbm, v_hbm, f_out, x_out,
           f, x, v0, v1, r, x1, fb, fbt, xh0, xl0, xh1, xl1, xr, gs, gr, lo0, hi0, coef, lags, weights, mask,
           load_sem, out_sem, send_sem, recv_sem, hsend_sem, hrecv_sem):
    block_len = x.shape[0]
    rows = f.shape[0]
    count = block_len // CHUNK
    order = chunk_order(count)
    last = block_len - HALO
    blocks = strata * groups
    s = lax.axis_index("stratum")
    g = lax.axis_index("tm")
    c = s * groups + g
    cr = lax.rem(c + 1, blocks)
    cl = lax.rem(c + blocks - 1, blocks)
    right = (cr // groups, lax.rem(cr, groups))
    left = (cl // groups, lax.rem(cl, groups))
    nxt = (lax.rem(s + 1, strata), g)
    prv = (lax.rem(s + strata - 1, strata), g)

    def cols(j):
        return pl.ds(j * CHUNK, CHUNK)

    def inner(j):
        return pl.ds(HALO + j * CHUNK, CHUNK)

    load_x = pltpu.make_async_copy(x_hbm, x, load_sem.at[0])
    load_f = pltpu.make_async_copy(f_hbm, f, load_sem.at[1])
    load_v1 = pltpu.make_async_copy(v_hbm.at[1], v1, load_sem.at[2])
    load_v0 = {
        j: pltpu.make_async_copy(v_hbm.at[0, :, cols(j)], v0.at[:, cols(j)], load_sem.at[3 + j])
        for j in order
    }
    smalls = [
        pltpu.make_async_copy(source, here, load_sem.at[3 + count + at])
        for at, (source, here) in enumerate(((lags_hbm, lags), (weights_hbm, weights), (mask_hbm, mask)))
    ]
    for small in smalls:
        small.start()
    load_x.start()
    load_f.start()
    for j in order:
        load_v0[j].start()

    barrier = pltpu.get_barrier_semaphore()
    for peer in (left, right, nxt, prv):
        pl.semaphore_signal(barrier, inc=1, device_id=peer, device_id_type=MESH)
    pl.semaphore_wait(barrier, 4)

    def rim(source, target, at, peer):
        return pltpu.make_async_remote_copy(
            src_ref=source, dst_ref=target, send_sem=hsend_sem.at[at],
            recv_sem=hrecv_sem.at[at], device_id=peer, device_id_type=MESH)

    rim0_r = rim(x_hbm.at[pl.ds(last, HALO)], lo0, 0, right)
    rim0_l = rim(x_hbm.at[pl.ds(0, HALO)], hi0, 1, left)
    rim1_r = rim(xh1.at[pl.ds(block_len, HALO)], xh1.at[pl.ds(0, HALO)], 2, right)
    rim1_l = rim(xh1.at[pl.ds(HALO, HALO)], xh1.at[pl.ds(HALO + block_len, HALO)], 3, left)
    rim0_r.start()
    rim0_l.start()
    forth = {
        j: pltpu.make_async_remote_copy(
            src_ref=xh1.at[inner(j)], dst_ref=xr.at[cols(j)], send_sem=send_sem.at[j],
            recv_sem=recv_sem.at[j], device_id=nxt, device_id_type=MESH)
        for j in order
    }
    back = {
        j: pltpu.make_async_remote_copy(
            src_ref=gs.at[j], dst_ref=gr.at[j], send_sem=send_sem.at[count + j],
            recv_sem=recv_sem.at[count + j], device_id=prv, device_id_type=MESH)
        for j in order
    }

    for small in smalls:
        small.wait()
    lag = [lags[which] for which in range(LAGS)]
    weight = [weights[which] for which in range(LAGS)]
    step = lax.broadcasted_iota(jnp.int32, (BAND, BAND + 2 * HALO), 0)
    offset = lax.broadcasted_iota(jnp.int32, (BAND, BAND + 2 * HALO), 1) - HALO - step
    behind = jnp.where(offset == 0, 1.0, 0.0)
    for which in range(LAGS):
        behind = behind - jnp.where(offset == -lag[which], weight[which], 0.0)
    usual, final = behind, behind
    for which in range(LAGS):
        ahead = jnp.where(offset == lag[which], weight[which], 0.0)
        for other in range(LAGS):
            ahead = ahead - jnp.where(
                offset == lag[which] - lag[other], weight[which] * weight[other], 0.0)
        usual = usual - ahead
        held = (step + lag[which] < BAND) | (c < blocks - 1)
        final = final - jnp.where(held, ahead, 0.0)
    for at, matrix in enumerate((usual, final)):
        high = matrix.astype(jnp.bfloat16)
        coef[2 * at] = high
        coef[2 * at + 1] = (matrix - high.astype(jnp.float32)).astype(jnp.bfloat16)

    def split(value, high_ref, low_ref, at, size):
        high = value.astype(jnp.bfloat16)
        high_ref[pl.ds(at, size), :] = high
        low_ref[pl.ds(at, size), :] = (value - high.astype(jnp.float32)).astype(jnp.bfloat16)

    def lag_grad(high_ref, low_ref, j):
        bands = []
        for band in range(j * CHUNK // BAND, (j + 1) * CHUNK // BAND):
            near = pl.ds(band * BAND, BAND + 2 * HALO)
            at = 2 if band == block_len // BAND - 1 else 0
            high = high_ref[near, :]
            bands.append(
                jnp.dot(coef[at], high, preferred_element_type=jnp.float32)
                + jnp.dot(coef[at], low_ref[near, :], preferred_element_type=jnp.float32)
                + jnp.dot(coef[at + 1], high, preferred_element_type=jnp.float32))
        return jnp.concatenate(bands, axis=0)

    def chunk_grad(k, j, times, v):
        for band in range(rows // CHUNK):
            product = lax.dot_general(
                fb[pl.ds(band * CHUNK, CHUNK), :], times, NT, preferred_element_type=jnp.float32)
            for i in range(CHUNK // TILE):
                for l in range(CHUNK // TILE):
                    mark = mask[k, band * (CHUNK // TILE) + i, j * (CHUNK // TILE) + l].astype(jnp.float32)
                    here = (pl.ds(band * CHUNK + i * TILE, TILE), pl.ds(j * CHUNK + l * TILE, TILE))
                    tile = product[i * TILE:(i + 1) * TILE, l * TILE:(l + 1) * TILE]
                    r[here] = ((v[here].astype(jnp.float32) - tile) * mark).astype(jnp.bfloat16)
        grad = jnp.dot(fbt[...], r[:, cols(j)], preferred_element_type=jnp.float32)
        return grad.T

    def rows_step(times, base):
        for band in range(rows // CHUNK):
            here = pl.ds(band * CHUNK, CHUNK)
            grad = jnp.dot(
                r[here, :], times[pl.ds(base, block_len), :], preferred_element_type=jnp.float32)
            f[here, :] = f[here, :] + rate_rows * (grad - ridge_rows * f[here, :])

    def round_rows():
        for band in range(rows // CHUNK):
            here = pl.ds(band * CHUNK, CHUNK)
            low = f[here, :].astype(jnp.bfloat16)
            fb[here, :] = low
            fbt[:, here] = low.T

    def pack(grad, j):
        top = jnp.maximum(jnp.max(jnp.abs(grad), axis=0, keepdims=True), 1e-30)
        power = jnp.broadcast_to(jnp.ceil(jnp.log(top) * LOG2_E), (PAD, grad.shape[1]))
        per_unit = TOP * jnp.exp2(-power[:1, :])
        gs[j, pl.ds(0, CHUNK), :] = jnp.floor(grad * per_unit + 0.5).astype(jnp.int32).astype(jnp.int16)
        gs[j, pl.ds(CHUNK, PAD), :] = power.astype(jnp.int32).astype(jnp.int16)

    def unpack(j):
        power = gr[j, pl.ds(CHUNK, PAD), :].astype(jnp.int32).astype(jnp.float32)
        unit = (1.0 / TOP) * jnp.exp2(power[:1, :])
        return gr[j, pl.ds(0, CHUNK), :].astype(jnp.int32).astype(jnp.float32) * unit

    def ridge_step(now, high_ref, low_ref, j):
        return now - rate_time * (ridge_time * now + ridge_lags * lag_grad(high_ref, low_ref, j))

    load_f.wait()
    round_rows()
    load_x.wait()
    for j in range(count):
        split(x[cols(j), :], xh0, xl0, HALO + j * CHUNK, CHUNK)
    for j in order:
        load_v0[j].wait()
        grad = chunk_grad(0, j, xh0[inner(j), :], v0)
        if j == 0:
            rim0_r.wait_recv()
            split(jnp.where(c > 0, lo0[...], 0.0), xh0, xl0, 0, HALO)
        if j == count - 1:
            rim0_l.wait_recv()
            split(hi0[...], xh0, xl0, HALO + block_len, HALO)
        now = ridge_step(x[cols(j), :], xh0, xl0, j) + rate_time * grad
        x1[cols(j), :] = now
        split(now, xh1, xl1, HALO + j * CHUNK, CHUNK)
        forth[j].start()
        if j == order[0]:
            load_v1.start()
    rim1_r.start()
    rim1_l.start()
    rows_step(xh0, HALO)
    round_rows()

    load_v1.wait()
    for j in order:
        forth[j].wait_recv()
        grad = chunk_grad(1, j, xr[cols(j), :], v1)
        pack(grad, j)
        back[j].start()
        if j == 0:
            rim1_r.wait_recv()
            head = xh1[pl.ds(0, HALO), :]
            xh1[pl.ds(0, HALO), :] = jnp.where(c > 0, head, jnp.zeros_like(head))
            xl1[pl.ds(0, HALO), :] = jnp.zeros_like(head)
        if j == count - 1:
            rim1_l.wait_recv()
            xl1[pl.ds(HALO + block_len, HALO), :] = jnp.zeros((HALO, x.shape[1]), jnp.bfloat16)
        x[cols(j), :] = ridge_step(x1[cols(j), :], xh1, xl1, j)
    rows_step(xr, 0)
    store_f = pltpu.make_async_copy(f, f_out, out_sem.at[0])
    store_f.start()

    stores = []
    for j in order:
        back[j].wait_recv()
        x[cols(j), :] = x[cols(j), :] + rate_time * unpack(j)
        store = pltpu.make_async_copy(x.at[cols(j)], x_out.at[cols(j)], out_sem.at[1 + j])
        store.start()
        stores.append(store)
    for j in order:
        forth[j].wait_send()
        back[j].wait_send()
    for side in (rim0_r, rim0_l, rim1_r, rim1_l):
        side.wait_send()
    store_f.wait()
    for store in stores:
        store.wait()


def body(row_factors, time_factors, values, tile_mask, lags, ar_weights):
    strata = lax.axis_size("stratum")
    groups = lax.axis_size("tm")
    block_len, rank = time_factors.shape
    rows = row_factors.shape[0]
    count = block_len // CHUNK
    f32, bf16 = jnp.float32, jnp.bfloat16
    anywhere = pl.BlockSpec(memory_space=pl.ANY)
    return tuple(pl.pallas_call(
        functools.partial(kernel, strata, groups),
        out_shape=(
            jax.ShapeDtypeStruct((rows, rank), f32),
            jax.ShapeDtypeStruct((block_len, rank), f32),
        ),
        in_specs=[pl.BlockSpec(memory_space=pltpu.HBM)] * 6,
        out_specs=(anywhere, anywhere),
        scratch_shapes=[
            pltpu.VMEM((rows, rank), f32),
            pltpu.VMEM((block_len, rank), f32),
            pltpu.VMEM((rows, block_len), bf16),
            pltpu.VMEM((rows, block_len), bf16),
            pltpu.VMEM((rows, block_len), bf16),
            pltpu.VMEM((block_len, rank), f32),
            pltpu.VMEM((rows, rank), bf16),
            pltpu.VMEM((rank, rows), bf16),
            pltpu.VMEM((block_len + 2 * HALO, rank), bf16),
            pltpu.VMEM((block_len + 2 * HALO, rank), bf16),
            pltpu.VMEM((block_len + 2 * HALO, rank), bf16),
            pltpu.VMEM((block_len + 2 * HALO, rank), bf16),
            pltpu.VMEM((block_len, rank), bf16),
            pltpu.VMEM((count, CHUNK + PAD, rank), jnp.int16),
            pltpu.VMEM((count, CHUNK + PAD, rank), jnp.int16),
            pltpu.VMEM((HALO, rank), f32),
            pltpu.VMEM((HALO, rank), f32),
            pltpu.VMEM((4, BAND, BAND + 2 * HALO), bf16),
            pltpu.SMEM((LAGS,), jnp.int32),
            pltpu.SMEM((LAGS,), f32),
            pltpu.SMEM(tile_mask.shape, jnp.int32),
            pltpu.SemaphoreType.DMA((6 + count,)),
            pltpu.SemaphoreType.DMA((1 + count,)),
            pltpu.SemaphoreType.DMA((2 * count,)),
            pltpu.SemaphoreType.DMA((2 * count,)),
            pltpu.SemaphoreType.DMA((4,)),
            pltpu.SemaphoreType.DMA((4,)),
        ],
        compiler_params=pltpu.CompilerParams(
            collective_id=0, has_side_effects=True, vmem_limit_bytes=40 * 2**20),
    )(lags, ar_weights, tile_mask, row_factors, time_factors, values))


def solution(mesh):
    return jax.shard_map(
        body,
        mesh=mesh,
        in_specs=(
            P(("stratum", "tm"), None),
            P(("stratum", "tm"), None),
            P(None, ("stratum", "tm"), None),
            P(None, ("stratum", "tm"), None),
            P(),
            P(),
        ),
        out_specs=(P(("stratum", "tm"), None), P(("stratum", "tm"), None)),
        check_vma=False,
    )
```

```python
import functools

import jax
import jax.numpy as jnp
from jax import lax
from jax.experimental import pallas as pl
from jax.experimental.pallas import tpu as pltpu
from jax.sharding import PartitionSpec as P

HALO = 64
LAGS = 4
TILE = 128
CHUNK = 128
BAND = 128
PAD = 16
PARTS = 4
TOP = 32000.0
LOG2_E = 1.4426950408889634

rate_rows = 0.005
rate_time = 0.02
ridge_rows = 16.0
ridge_time = 2.0
ridge_lags = 8.0

MESH = pl.DeviceIdType.MESH
NT = (((1,), (1,)), ((), ()))


def chunk_order(count):
    inner = list(range(1, count - 1))
    return inner + [0, count - 1] if count > 1 else [0]


def kernel(strata, groups, lags_hbm, weights_hbm, mask_hbm, f_hbm, x_hbm, v_hbm, f_out, x_out,
           f, x, v0, v1, r, x1, fb, fbt, xh0, xl0, xh1, xl1, xr, gs, gr, lo0, hi0, coef, lags, weights, mask,
           load_sem, out_sem, send_sem, recv_sem, hsend_sem, hrecv_sem):
    block_len = x.shape[0]
    rows = f.shape[0]
    count = block_len // CHUNK
    order = chunk_order(count)
    last = block_len - HALO
    blocks = strata * groups
    s = lax.axis_index("stratum")
    g = lax.axis_index("tm")
    c = s * groups + g
    cr = lax.rem(c + 1, blocks)
    cl = lax.rem(c + blocks - 1, blocks)
    right = (cr // groups, lax.rem(cr, groups))
    left = (cl // groups, lax.rem(cl, groups))
    nxt = (lax.rem(s + 1, strata), g)
    prv = (lax.rem(s + strata - 1, strata), g)

    def cols(j):
        return pl.ds(j * CHUNK, CHUNK)

    def inner(j):
        return pl.ds(HALO + j * CHUNK, CHUNK)

    load_x = pltpu.make_async_copy(x_hbm, x, load_sem.at[0])
    load_f = pltpu.make_async_copy(f_hbm, f, load_sem.at[1])
    load_v1 = pltpu.make_async_copy(v_hbm.at[1], v1, load_sem.at[2])
    load_v0 = {
        j: pltpu.make_async_copy(v_hbm.at[0, :, cols(j)], v0.at[:, cols(j)], load_sem.at[3 + j])
        for j in order
    }
    smalls = [
        pltpu.make_async_copy(source, here, load_sem.at[3 + count + at])
        for at, (source, here) in enumerate(((lags_hbm, lags), (weights_hbm, weights), (mask_hbm, mask)))
    ]
    for small in smalls:
        small.start()
    load_x.start()
    load_f.start()
    for j in order:
        load_v0[j].start()

    barrier = pltpu.get_barrier_semaphore()
    for peer in (left, right, nxt, prv):
        pl.semaphore_signal(barrier, inc=1, device_id=peer, device_id_type=MESH)

    def rim(source, target, at, peer):
        return pltpu.make_async_remote_copy(
            src_ref=source, dst_ref=target, send_sem=hsend_sem.at[at],
            recv_sem=hrecv_sem.at[at], device_id=peer, device_id_type=MESH)

    rim0_r = rim(x_hbm.at[pl.ds(last, HALO)], lo0, 0, right)
    rim0_l = rim(x_hbm.at[pl.ds(0, HALO)], hi0, 1, left)
    rim1_r = rim(xh1.at[pl.ds(block_len, HALO)], xh1.at[pl.ds(0, HALO)], 2, right)
    rim1_l = rim(xh1.at[pl.ds(HALO, HALO)], xh1.at[pl.ds(HALO + block_len, HALO)], 3, left)
    forth = {
        j: pltpu.make_async_remote_copy(
            src_ref=xh1.at[inner(j)], dst_ref=xr.at[cols(j)], send_sem=send_sem.at[j],
            recv_sem=recv_sem.at[j], device_id=nxt, device_id_type=MESH)
        for j in order
    }
    back = {
        j: pltpu.make_async_remote_copy(
            src_ref=gs.at[j], dst_ref=gr.at[j], send_sem=send_sem.at[count + j],
            recv_sem=recv_sem.at[count + j], device_id=prv, device_id_type=MESH)
        for j in order
    }

    for small in smalls:
        small.wait()
    lag = [lags[which] for which in range(LAGS)]
    weight = [weights[which] for which in range(LAGS)]
    step = lax.broadcasted_iota(jnp.int32, (BAND, BAND + 2 * HALO), 0)
    offset = lax.broadcasted_iota(jnp.int32, (BAND, BAND + 2 * HALO), 1) - HALO - step
    behind = jnp.where(offset == 0, 1.0, 0.0)
    for which in range(LAGS):
        behind = behind - jnp.where(offset == -lag[which], weight[which], 0.0)
    usual, final = behind, behind
    for which in range(LAGS):
        ahead = jnp.where(offset == lag[which], weight[which], 0.0)
        for other in range(LAGS):
            ahead = ahead - jnp.where(
                offset == lag[which] - lag[other], weight[which] * weight[other], 0.0)
        usual = usual - ahead
        held = (step + lag[which] < BAND) | (c < blocks - 1)
        final = final - jnp.where(held, ahead, 0.0)
    for at, matrix in enumerate((usual, final)):
        high = matrix.astype(jnp.bfloat16)
        coef[2 * at] = high
        coef[2 * at + 1] = (matrix - high.astype(jnp.float32)).astype(jnp.bfloat16)

    def split(value, high_ref, low_ref, at, size):
        high = value.astype(jnp.bfloat16)
        high_ref[pl.ds(at, size), :] = high
        low_ref[pl.ds(at, size), :] = (value - high.astype(jnp.float32)).astype(jnp.bfloat16)

    def lag_grad(high_ref, low_ref, j):
        bands = []
        for band in range(j * CHUNK // BAND, (j + 1) * CHUNK // BAND):
            near = pl.ds(band * BAND, BAND + 2 * HALO)
            at = 2 if band == block_len // BAND - 1 else 0
            high = high_ref[near, :]
            bands.append(
                jnp.dot(coef[at], high, preferred_element_type=jnp.float32)
                + jnp.dot(coef[at], low_ref[near, :], preferred_element_type=jnp.float32)
                + jnp.dot(coef[at + 1], high, preferred_element_type=jnp.float32))
        return jnp.concatenate(bands, axis=0)

    def chunk_grad(k, j, times, v):
        for band in range(rows // CHUNK):
            product = lax.dot_general(
                fb[pl.ds(band * CHUNK, CHUNK), :], times, NT, preferred_element_type=jnp.float32)
            for i in range(CHUNK // TILE):
                for l in range(CHUNK // TILE):
                    mark = mask[k, band * (CHUNK // TILE) + i, j * (CHUNK // TILE) + l].astype(jnp.float32)
                    here = (pl.ds(band * CHUNK + i * TILE, TILE), pl.ds(j * CHUNK + l * TILE, TILE))
                    tile = product[i * TILE:(i + 1) * TILE, l * TILE:(l + 1) * TILE]
                    r[here] = ((v[here].astype(jnp.float32) - tile) * mark).astype(jnp.bfloat16)
        grad = jnp.dot(fbt[...], r[:, cols(j)], preferred_element_type=jnp.float32)
        return grad.T

    def rows_step(times, base):
        for band in range(rows // CHUNK):
            here = pl.ds(band * CHUNK, CHUNK)
            grad = jnp.dot(
                r[here, :], times[pl.ds(base, block_len), :], preferred_element_type=jnp.float32)
            f[here, :] = f[here, :] + rate_rows * (grad - ridge_rows * f[here, :])

    def round_rows():
        for band in range(rows // CHUNK):
            here = pl.ds(band * CHUNK, CHUNK)
            low = f[here, :].astype(jnp.bfloat16)
            fb[here, :] = low
            fbt[:, here] = low.T

    def pack(grad, j):
        top = jnp.maximum(jnp.max(jnp.abs(grad), axis=0, keepdims=True), 1e-30)
        power = jnp.broadcast_to(jnp.ceil(jnp.log(top) * LOG2_E), (PAD, grad.shape[1]))
        per_unit = TOP * jnp.exp2(-power[:1, :])
        gs[j, pl.ds(0, CHUNK), :] = jnp.floor(grad * per_unit + 0.5).astype(jnp.int32).astype(jnp.int16)
        gs[j, pl.ds(CHUNK, PAD), :] = power.astype(jnp.int32).astype(jnp.int16)

    def unpack(j):
        power = gr[j, pl.ds(CHUNK, PAD), :].astype(jnp.int32).astype(jnp.float32)
        unit = (1.0 / TOP) * jnp.exp2(power[:1, :])
        return gr[j, pl.ds(0, CHUNK), :].astype(jnp.int32).astype(jnp.float32) * unit

    def ridge_step(now, high_ref, low_ref, j):
        return now - rate_time * (ridge_time * now + ridge_lags * lag_grad(high_ref, low_ref, j))

    load_f.wait()
    round_rows()
    load_x.wait()
    for j in range(count):
        split(x[cols(j), :], xh0, xl0, HALO + j * CHUNK, CHUNK)
    for j in order:
        load_v0[j].wait()
        grad = chunk_grad(0, j, xh0[inner(j), :], v0)
        if j == 0:
            rim0_r.wait_recv()
            split(jnp.where(c > 0, lo0[...], 0.0), xh0, xl0, 0, HALO)
        if j == count - 1:
            rim0_l.wait_recv()
            split(hi0[...], xh0, xl0, HALO + block_len, HALO)
        now = ridge_step(x[cols(j), :], xh0, xl0, j) + rate_time * grad
        x1[cols(j), :] = now
        split(now, xh1, xl1, HALO + j * CHUNK, CHUNK)
        if j == order[0]:
            pl.semaphore_wait(barrier, 4)
            rim0_r.start()
            rim0_l.start()
        forth[j].start()
        if j == order[0]:
            load_v1.start()
    rim1_r.start()
    rim1_l.start()
    rows_step(xh0, HALO)
    round_rows()

    load_v1.wait()
    for j in order:
        forth[j].wait_recv()
        grad = chunk_grad(1, j, xr[cols(j), :], v1)
        pack(grad, j)
        back[j].start()
        if j == 0:
            rim1_r.wait_recv()
            head = xh1[pl.ds(0, HALO), :]
            xh1[pl.ds(0, HALO), :] = jnp.where(c > 0, head, jnp.zeros_like(head))
            xl1[pl.ds(0, HALO), :] = jnp.zeros_like(head)
        if j == count - 1:
            rim1_l.wait_recv()
            xl1[pl.ds(HALO + block_len, HALO), :] = jnp.zeros((HALO, x.shape[1]), jnp.bfloat16)
        x[cols(j), :] = ridge_step(x1[cols(j), :], xh1, xl1, j)
    rows_step(xr, 0)
    store_f = pltpu.make_async_copy(f, f_out, out_sem.at[0])
    store_f.start()

    stores = []
    for j in order:
        back[j].wait_recv()
        x[cols(j), :] = x[cols(j), :] + rate_time * unpack(j)
        store = pltpu.make_async_copy(x.at[cols(j)], x_out.at[cols(j)], out_sem.at[1 + j])
        store.start()
        stores.append(store)
    for j in order:
        forth[j].wait_send()
        back[j].wait_send()
    for side in (rim0_r, rim0_l, rim1_r, rim1_l):
        side.wait_send()
    store_f.wait()
    for store in stores:
        store.wait()


def hand_over(f_in, x_in, f_out, x_out, held, in_sem, out_sem):
    loads, stores = [], []
    for at, (source, target) in enumerate(((f_in, f_out), (x_in, x_out))):
        size = source.shape[0] // PARTS
        for part in range(PARTS):
            here = pl.ds(part * size, size)
            loads.append(pltpu.make_async_copy(source.at[here], held.at[at, here], in_sem.at[at, part]))
            stores.append(pltpu.make_async_copy(held.at[at, here], target.at[here], out_sem.at[at, part]))
    for load in loads:
        load.start()
    for load, store in zip(loads, stores):
        load.wait()
        store.start()
    for store in stores:
        store.wait()


def body(row_factors, time_factors, values, tile_mask, lags, ar_weights):
    strata = lax.axis_size("stratum")
    groups = lax.axis_size("tm")
    block_len, rank = time_factors.shape
    rows = row_factors.shape[0]
    count = block_len // CHUNK
    f32, bf16 = jnp.float32, jnp.bfloat16
    anywhere = pl.BlockSpec(memory_space=pl.ANY)
    updated = pl.pallas_call(
        functools.partial(kernel, strata, groups),
        out_shape=(
            jax.ShapeDtypeStruct((rows, rank), f32),
            jax.ShapeDtypeStruct((block_len, rank), f32),
        ),
        in_specs=[pl.BlockSpec(memory_space=pltpu.HBM)] * 6,
        out_specs=(anywhere, anywhere),
        scratch_shapes=[
            pltpu.VMEM((rows, rank), f32),
            pltpu.VMEM((block_len, rank), f32),
            pltpu.VMEM((rows, block_len), bf16),
            pltpu.VMEM((rows, block_len), bf16),
            pltpu.VMEM((rows, block_len), bf16),
            pltpu.VMEM((block_len, rank), f32),
            pltpu.VMEM((rows, rank), bf16),
            pltpu.VMEM((rank, rows), bf16),
            pltpu.VMEM((block_len + 2 * HALO, rank), bf16),
            pltpu.VMEM((block_len + 2 * HALO, rank), bf16),
            pltpu.VMEM((block_len + 2 * HALO, rank), bf16),
            pltpu.VMEM((block_len + 2 * HALO, rank), bf16),
            pltpu.VMEM((block_len, rank), bf16),
            pltpu.VMEM((count, CHUNK + PAD, rank), jnp.int16),
            pltpu.VMEM((count, CHUNK + PAD, rank), jnp.int16),
            pltpu.VMEM((HALO, rank), f32),
            pltpu.VMEM((HALO, rank), f32),
            pltpu.VMEM((4, BAND, BAND + 2 * HALO), bf16),
            pltpu.SMEM((LAGS,), jnp.int32),
            pltpu.SMEM((LAGS,), f32),
            pltpu.SMEM(tile_mask.shape, jnp.int32),
            pltpu.SemaphoreType.DMA((6 + count,)),
            pltpu.SemaphoreType.DMA((1 + count,)),
            pltpu.SemaphoreType.DMA((2 * count,)),
            pltpu.SemaphoreType.DMA((2 * count,)),
            pltpu.SemaphoreType.DMA((4,)),
            pltpu.SemaphoreType.DMA((4,)),
        ],
        compiler_params=pltpu.CompilerParams(
            collective_id=0, has_side_effects=True, vmem_limit_bytes=60 * 2**20),
    )(lags, ar_weights, tile_mask, row_factors, time_factors, values)
    return tuple(pl.pallas_call(
        hand_over,
        out_shape=tuple(jax.ShapeDtypeStruct(array.shape, array.dtype) for array in updated),
        in_specs=[anywhere] * 2,
        out_specs=(anywhere, anywhere),
        scratch_shapes=[
            pltpu.VMEM((2, rows, rank), f32),
            pltpu.SemaphoreType.DMA((2, PARTS)),
            pltpu.SemaphoreType.DMA((2, PARTS)),
        ],
        compiler_params=pltpu.CompilerParams(vmem_limit_bytes=60 * 2**20),
    )(*updated))


def solution(mesh):
    return jax.shard_map(
        body,
        mesh=mesh,
        in_specs=(
            P(("stratum", "tm"), None),
            P(("stratum", "tm"), None),
            P(None, ("stratum", "tm"), None),
            P(None, ("stratum", "tm"), None),
            P(),
            P(),
        ),
        out_specs=(P(("stratum", "tm"), None), P(("stratum", "tm"), None)),
        check_vma=False,
    )
```
